32 devices in a mesh: group: 2 (over x), feat: 16 (over z, y, core).
Axes of the slice: x: 2, y: 2, z: 4, core: 2. Of those that a mesh axis runs over, the one named last changes fastest.
Arguments:
- store_inputs: bfloat16 [2, 512, 2048], P(None, ('group', 'feat')), parts along dimension 1, may hold values from -6 to 6
- store_targets: bfloat16 [2, 512, 2048], P(None, ('group', 'feat')), parts along dimension 1, may hold values from -6 to 6
- row_ids: int32 [256], P(('group', 'feat')), parts along dimension 0, may hold values from 0 to 15
- enc_weight: bfloat16 [2, 2048, 16384], P(None, None, 'feat'), may hold values from -0.125 to 0.125
- enc_bias: float32 [2, 16384], P(None, 'feat'), may hold values from -3 to 3
- dec_weight: bfloat16 [3, 16384, 2048], P(None, 'feat'), may hold values from -0.046875 to 0.046875
Outputs:
- enc_grad: bfloat16 [4, 2048, 16384], P('group', None, 'feat'), parts along dimension 0
- bias_grad: float32 [4, 16384], P('group', 'feat'), parts along dimension 0
- dec_grad: bfloat16 [6, 16384, 2048], P('group', 'feat'), parts along dimension 0
The draws below stay inside these ranges and needn't reach their ends.
There are 2 independent parts, one for each index of `group`. The reference program is written for one: setup_inputs(seed, part) draws one part's arguments, and reference() takes and returns one part's arrays. A program takes and returns all parts, laid end to end along the dimension named above; an argument that names none is the same for every part. Nothing has to cross between parts.
Inputs may be any that keep to these rules, and one draw needn't show every extreme that they name: row_ids[i] indexes the store rows held with token i, as in the first step.
All inputs are finite; a program needn't handle non-finite values.
Results may differ from the reference program's by a relative error of at most 0.035.
Values may be sent and summed in bfloat16 or wider, within the bound.
A program may use at most 128 MiB of HBM per device.

```python
import math
import jax
import jax.numpy as jnp
from jax import lax

D = 2048
F = 16384
L = 2
TOK_DEV = 8
PAIRS = 3
BUF_DEV = 16
TOKENS = 128
BUF = 256


def plant(array, rng, least, largest):
    place = [jax.random.randint(jax.random.fold_in(rng, axis), (), 0, length) for axis, length in enumerate(array.shape)]
    widest = array.shape.index(max(array.shape))
    beside = place[:widest] + [(place[widest] + 1) % array.shape[widest]] + place[widest + 1:]
    return array.at[tuple(place)].set(least).at[tuple(beside)].set(largest)


def level_of(stream_key, dims, pieces, smallest, largest):
    gain = 1.0
    for axis_at, blocks in pieces:
        heights = jax.random.uniform(jax.random.fold_in(jax.random.fold_in(stream_key, 6), axis_at), (blocks,), jnp.float32, smallest / len(pieces), largest / len(pieces))
        gain = gain * jnp.repeat(jnp.exp(heights), dims[axis_at] // blocks).reshape((-1,) + (1,) * (len(dims) - 1 - axis_at))
    return gain


def normal_values(rng, dims, deviation, reach, split=(), held_as=jnp.bfloat16):
    array = deviation * jax.random.normal(rng, dims, jnp.float32)
    if split:
        array = array * level_of(rng, dims, split, -0.22, 0.18)
    return jnp.clip(array, -reach, reach).astype(held_as)


def setup_inputs(seed: int = 0, part: int = 0) -> dict:
    splits = jax.random.split(jax.random.key(seed), 7)
    part_keys = jax.random.split(jax.random.fold_in(splits[6], part), 7)
    return {
        "store_inputs": normal_values(part_keys[0], (L, BUF, D), 1.0, 6.0, ((1, 16),)),
        "store_targets": normal_values(part_keys[1], (L, BUF, D), 1.0, 6.0, ((1, 16),)),
        "row_ids": plant(jax.random.randint(part_keys[2], (TOKENS,), 0, BUF_DEV), jax.random.fold_in(part_keys[2], 1), 0, BUF_DEV - 1).astype(jnp.int32),
        "enc_weight": normal_values(splits[3], (L, D, F), D ** -0.5, 0.125, ((2, 16),)),
        "enc_bias": normal_values(splits[4], (L, F), 0.5, 3.0, ((1, 16),), jnp.float32),
        "dec_weight": normal_values(splits[5], (PAIRS, F, D), F ** -0.5, 0.046875, ((1, 16),)),
    }


def reference(store_inputs, store_targets, row_ids, enc_weight, enc_bias, dec_weight):
    row_index = jnp.arange(TOKENS, dtype=jnp.int32) // TOK_DEV * BUF_DEV + row_ids.astype(jnp.int32)
    inputs = jnp.take(store_inputs, row_index, axis=1)
    targets = jnp.take(store_targets, row_index, axis=1)
    grad_scale = 1.0 / math.sqrt(TOKENS)
    pair_list = [(source, target) for source in range(L) for target in range(source, L)]
    preact = [jnp.dot(inputs[index], enc_weight[index], preferred_element_type=jnp.float32) + enc_bias[index] for index in range(L)]
    features = [jnp.maximum(value, 0.0).astype(jnp.bfloat16) for value in preact]
    errors = []
    for target in range(L):
        rebuilt = jnp.zeros((TOKENS, D), jnp.float32)
        for index, (source, goal) in enumerate(pair_list):
            if goal == target:
                rebuilt = rebuilt + jnp.dot(features[source], dec_weight[index], preferred_element_type=jnp.float32)
        errors.append((rebuilt - targets[target].astype(jnp.float32)).astype(jnp.bfloat16))
    dec_list = []
    feature_grad = [jnp.zeros((TOKENS, F), jnp.float32) for index in range(L)]
    for index, (source, target) in enumerate(pair_list):
        product = jnp.dot(features[source].T, errors[target], preferred_element_type=jnp.float32)
        dec_list.append((grad_scale * product).astype(jnp.bfloat16))
        feature_grad[source] = feature_grad[source] + lax.dot_general(errors[target], dec_weight[index], (((1,), (1,)), ((), ())), preferred_element_type=jnp.float32)
    enc_list = []
    bias_list = []
    for index in range(L):
        pre_grad = jnp.where(preact[index] > 0, feature_grad[index], 0.0) * grad_scale
        bias_list.append(lax.optimization_barrier(jnp.sum(pre_grad, axis=0)))
        enc_list.append(jnp.dot(inputs[index].T, pre_grad.astype(jnp.bfloat16), preferred_element_type=jnp.float32).astype(jnp.bfloat16))
    return (jnp.stack(enc_list), jnp.stack(bias_list), jnp.stack(dec_list))
```

```python
import functools
import math

import jax
import jax.numpy as jnp
from jax import lax
from jax.experimental import pallas as pl
from jax.experimental.pallas import tpu as pltpu
from jax.sharding import PartitionSpec as P

BF = jnp.bfloat16
F32 = jnp.float32


def place(n):
    me = lax.axis_index("feat")
    return me // 4, (me // 2) % 2, me % 2


def index_of(z, y, c):
    return (z * 2 + y) * 2 + c


def near_first(depth):
    return sorted(range(1, depth), key=lambda k: min(k, depth - k))


def greet(n):
    depth = n // 4
    z, y, c = place(n)
    barrier = pltpu.get_barrier_semaphore()
    peers = [index_of(z, y, 1 - c), index_of(z, 1 - y, c)]
    peers += [index_of((z + k) % depth, y, c) for k in range(1, depth)]
    for peer in peers:
        pl.semaphore_signal(
            barrier, inc=1, device_id={"feat": peer}, device_id_type=pl.DeviceIdType.MESH
        )
    pl.semaphore_wait(barrier, len(peers))


def send(src, dst, send_sem, recv_sem, peer):
    return pltpu.make_async_remote_copy(
        src_ref=src,
        dst_ref=dst,
        send_sem=send_sem,
        recv_sem=recv_sem,
        device_id={"feat": peer},
        device_id_type=pl.DeviceIdType.MESH,
    )


def spread(n, buf, zs, zr, ys, yr, cs, cr):
    depth = n // 4
    z, y, c = place(n)
    core, side = index_of(z, y, 1 - c), index_of(z, 1 - y, c)
    started = []

    def go(chunk, send_sem, recv_sem, peer):
        copy = send(buf.at[chunk], buf.at[chunk], send_sem, recv_sem, peer)
        copy.start()
        started.append(copy)

    def arrive(chunk, send_sem, recv_sem, peer):
        send(buf.at[chunk], buf.at[chunk], send_sem, recv_sem, peer).wait_recv()

    order = near_first(depth)
    mine = index_of(z, y, c)
    go(mine, ys.at[0], yr.at[0], side)
    for k in reversed(order):
        go(mine, zs.at[k], zr.at[k], index_of((z + k) % depth, y, c))
    go(mine, cs.at[0], cr.at[0], core)
    for k in order:
        chunk = index_of((z - k + depth) % depth, y, c)
        arrive(chunk, zs.at[k], zr.at[k], core)
        go(chunk, ys.at[k], yr.at[k], side)
        go(chunk, cs.at[k], cr.at[k], core)
    for k in [0] + order:
        chunk = index_of((z - k + depth) % depth, 1 - y, c)
        arrive(chunk, ys.at[k], yr.at[k], side)
        go(chunk, cs.at[depth + k], cr.at[depth + k], core)
    for k in [0] + order:
        arrive(index_of((z - k + depth) % depth, y, 1 - c), cs.at[k], cr.at[k], core)
    for k in [0] + order:
        chunk = index_of((z - k + depth) % depth, 1 - y, 1 - c)
        arrive(chunk, cs.at[depth + k], cr.at[depth + k], core)
    for copy in started:
        copy.wait_send()


def gathered(n, layers, buf, out_ref):
    rows = buf.shape[1]
    width = out_ref.shape[2]
    for i in range(0, n, 2):
        for layer in range(layers):
            cols = pl.ds(layer * width, width)
            both = jnp.concatenate([buf[i, :, cols].astype(F32), buf[i + 1, :, cols].astype(F32)])
            out_ref[layer, pl.ds(i * rows, 2 * rows), :] = both.astype(BF)


def gather_kernel(n, layers, ids_ref, store_ref, out_ref, buf, *sems):
    width = store_ref.shape[2]
    me = lax.axis_index("feat")
    held = store_ref.shape[1]
    rows = ids_ref.shape[0]
    hot = (ids_ref[...] == lax.broadcasted_iota(jnp.int32, (rows, held), 1)).astype(BF)
    for layer in range(layers):
        picked = jnp.dot(hot, store_ref[layer], preferred_element_type=F32)
        buf[me, :, pl.ds(layer * width, width)] = picked.astype(BF)
    greet(n)
    spread(n, buf, *sems)
    gathered(n, layers, buf, out_ref)


def errors_kernel(
    n, layers, ids_ref, store_ref, part_ref, out_ref, buf, cst, yst, zst, cin, yin, zin,
    rcs, rcr, rys, ryr, rzs, rzr, *sems
):
    depth = n // 4
    width = store_ref.shape[2]
    held = store_ref.shape[1]
    rows = ids_ref.shape[0]
    z, y, c = place(n)
    core, side = index_of(z, y, 1 - c), index_of(z, 1 - y, c)
    order = near_first(depth)
    far = list(reversed(order)) + [0]
    started = []
    greet(n)

    def go(src, dst, send_sem, recv_sem, peer):
        copy = send(src, dst, send_sem, recv_sem, peer)
        copy.start()
        started.append(copy)

    def term(zz, yy, cc):
        index = index_of(zz, yy, cc)
        return [part_ref[layer, index] for layer in range(layers)]

    def keep(dst, slot, values):
        for layer in range(layers):
            dst[slot, :, pl.ds(layer * width, width)] = values[layer].astype(BF)

    def plus(values, src, slot):
        return [
            values[layer] + src[slot, :, pl.ds(layer * width, width)].astype(F32)
            for layer in range(layers)
        ]

    for j, yy in ((0, 1 - y), (1, y)):
        for k in far:
            slot = j * depth + k
            keep(cst, slot, term((z + k) % depth, yy, 1 - c))
            go(cst.at[slot], cin.at[slot], rcs.at[slot], rcr.at[slot], core)
    for k in far:
        send(cst.at[k], cin.at[k], rcs.at[k], rcr.at[k], core).wait_recv()
        keep(yst, k, plus(term((z + k) % depth, 1 - y, c), cin, k))
        go(yst.at[k], yin.at[k], rys.at[k], ryr.at[k], side)
    hot = (ids_ref[...] == lax.broadcasted_iota(jnp.int32, (rows, held), 1)).astype(BF)
    targets = [jnp.dot(hot, store_ref[layer], preferred_element_type=F32) for layer in range(layers)]
    for k in far:
        slot = depth + k
        send(cst.at[slot], cin.at[slot], rcs.at[slot], rcr.at[slot], core).wait_recv()
        send(yst.at[k], yin.at[k], rys.at[k], ryr.at[k], side).wait_recv()
        total = plus(plus(term((z + k) % depth, y, c), cin, slot), yin, k)
        if k:
            keep(zst, k, total)
            go(zst.at[k], zin.at[k], rzs.at[k], rzr.at[k], index_of((z + k) % depth, y, c))
    for k in order:
        send(zst.at[k], zin.at[k], rzs.at[k], rzr.at[k], core).wait_recv()
        total = plus(total, zin, k)
    keep(buf, index_of(z, y, c), [total[layer] - targets[layer] for layer in range(layers)])
    for copy in started:
        copy.wait_send()
    spread(n, buf, *sems)
    gathered(n, layers, buf, out_ref)


def gather_sems(depth):
    dma = pltpu.SemaphoreType.DMA
    return [dma((depth,))] * 4 + [dma((2 * depth,))] * 2


VMEM = pl.BlockSpec(memory_space=pltpu.VMEM)


def gather_inputs(n, ids, store):
    layers, _, width = store.shape
    rows = ids.shape[0]
    return pl.pallas_call(
        functools.partial(gather_kernel, n, layers),
        out_shape=jax.ShapeDtypeStruct((layers, n * rows, width), BF),
        in_specs=[VMEM] * 2,
        out_specs=VMEM,
        scratch_shapes=[pltpu.VMEM((n, rows, layers * width), BF)] + gather_sems(n // 4),
        compiler_params=pltpu.CompilerParams(collective_id=0, has_side_effects=True),
        name="gather_inputs",
    )(ids, store)


def reduce_errors(n, ids, store, part):
    layers, _, width = store.shape
    rows = ids.shape[0]
    depth = n // 4
    dma = pltpu.SemaphoreType.DMA
    chunks = lambda count: pltpu.VMEM((count, rows, layers * width), BF)
    return pl.pallas_call(
        functools.partial(errors_kernel, n, layers),
        out_shape=jax.ShapeDtypeStruct((layers, n * rows, width), BF),
        in_specs=[VMEM] * 3,
        out_specs=VMEM,
        scratch_shapes=[chunks(n), chunks(2 * depth), chunks(depth), chunks(depth)]
        + [chunks(2 * depth), chunks(depth), chunks(depth)]
        + [dma((2 * depth,))] * 2
        + [dma((depth,))] * 4
        + gather_sems(depth),
        compiler_params=pltpu.CompilerParams(collective_id=1, has_side_effects=True),
        name="reduce_errors",
    )(ids, store, part)


def backward_kernel(pairs, scale, x_ref, e_ref, a_ref, w_ref, enc_ref, bias_ref, dec_ref, xt):
    layers = x_ref.shape[0]

    @pl.when(pl.program_id(0) == 0)
    def _():
        for layer in range(layers):
            xt[layer] = x_ref[layer].T

    for source in range(layers):
        active = a_ref[source]
        turned = jnp.maximum(active, 0.0).astype(BF).T
        grad = None
        for index, (first, target) in enumerate(pairs):
            if first != source:
                continue
            dec = jnp.dot(turned, e_ref[target], preferred_element_type=F32)
            dec_ref[index] = (scale * dec).astype(BF)
            back = lax.dot_general(
                e_ref[target], w_ref[index], (((1,), (1,)), ((), ())), preferred_element_type=F32
            )
            grad = back if grad is None else grad + back
        pre = jnp.where(active > 0, grad, 0.0) * scale
        bias_ref[pl.ds(source, 1), :] = jnp.sum(pre, axis=0, keepdims=True)
        enc = jnp.dot(xt[source], pre.astype(BF), preferred_element_type=F32)
        enc_ref[source] = enc.astype(BF)


def backward(pairs, scale, x, errors, preact, dec_weight):
    layers, tokens, width = x.shape
    features = preact.shape[2]
    tile = min(256, features)
    whole = pl.BlockSpec((layers, tokens, width), lambda i: (0, 0, 0))
    rows = pl.BlockSpec((len(pairs), tile, width), lambda i: (0, i, 0))
    return pl.pallas_call(
        functools.partial(backward_kernel, pairs, scale),
        grid=(features // tile,),
        out_shape=(
            jax.ShapeDtypeStruct((layers, width, features), BF),
            jax.ShapeDtypeStruct((layers, features), F32),
            jax.ShapeDtypeStruct((len(pairs), features, width), BF),
        ),
        in_specs=[whole, whole, pl.BlockSpec((layers, tokens, tile), lambda i: (0, 0, i)), rows],
        out_specs=(
            pl.BlockSpec((layers, width, tile), lambda i: (0, 0, i)),
            pl.BlockSpec((layers, tile), lambda i: (0, i)),
            rows,
        ),
        scratch_shapes=[pltpu.VMEM((layers, width, tokens), BF)],
        compiler_params=pltpu.CompilerParams(vmem_limit_bytes=48 * 1024 * 1024),
        name="backward",
    )(x, errors, preact, dec_weight)


def local(n, store_inputs, store_targets, row_ids, enc_weight, enc_bias, dec_weight):
    layers, width = enc_weight.shape[:2]
    rows = row_ids.shape[0]
    pairs = [(source, target) for source in range(layers) for target in range(source, layers)]
    scale = 1.0 / math.sqrt(rows * n)
    ids = row_ids.reshape(rows, 1)
    x = gather_inputs(n, ids, store_inputs)
    preact = [
        jnp.dot(x[layer], enc_weight[layer], preferred_element_type=F32) + enc_bias[layer]
        for layer in range(layers)
    ]
    features = [jnp.maximum(value, 0.0).astype(BF) for value in preact]
    part = []
    for target in range(layers):
        part.append(
            sum(
                jnp.dot(features[source], dec_weight[index], preferred_element_type=F32)
                for index, (source, goal) in enumerate(pairs)
                if goal == target
            )
        )
    part = jnp.stack(part).reshape(layers, n, rows, width)
    errors = reduce_errors(n, ids, store_targets, part)
    return backward(pairs, scale, x, errors, jnp.stack(preact), dec_weight)


def solution(mesh):
    in_specs = (
        P(None, ("group", "feat"), None),
        P(None, ("group", "feat"), None),
        P(("group", "feat")),
        P(None, None, "feat"),
        P(None, "feat"),
        P(None, "feat", None),
    )
    out_specs = (P("group", None, "feat"), P("group", "feat"), P("group", "feat", None))
    body = functools.partial(local, mesh.shape["feat"])
    return jax.shard_map(body, mesh=mesh, in_specs=in_specs, out_specs=out_specs, check_vma=False)
```

```python
import functools
import math

import jax
import jax.numpy as jnp
from jax import lax
from jax.experimental import pallas as pl
from jax.experimental.pallas import tpu as pltpu
from jax.sharding import PartitionSpec as P

BF = jnp.bfloat16
F32 = jnp.float32


def place(n):
    me = lax.axis_index("feat")
    return me // 4, (me // 2) % 2, me % 2


def index_of(z, y, c):
    return (z * 2 + y) * 2 + c


def near_first(depth):
    return sorted(range(1, depth), key=lambda k: min(k, depth - k))


def greet(n):
    depth = n // 4
    z, y, c = place(n)
    barrier = pltpu.get_barrier_semaphore()
    peers = [index_of(z, y, 1 - c), index_of(z, 1 - y, c)]
    peers += [index_of((z + k) % depth, y, c) for k in range(1, depth)]
    for peer in peers:
        pl.semaphore_signal(
            barrier, inc=1, device_id={"feat": peer}, device_id_type=pl.DeviceIdType.MESH
        )
    pl.semaphore_wait(barrier, len(peers))


def send(src, dst, send_sem, recv_sem, peer):
    return pltpu.make_async_remote_copy(
        src_ref=src,
        dst_ref=dst,
        send_sem=send_sem,
        recv_sem=recv_sem,
        device_id={"feat": peer},
        device_id_type=pl.DeviceIdType.MESH,
    )


def one_hot(ids_ref, rows, held):
    at = lax.broadcasted_iota(jnp.int32, (rows, held), 0)
    ids = jnp.zeros((rows, held), jnp.int32)
    for row in range(rows):
        ids = jnp.where(at == row, ids_ref[row], ids)
    return (ids == lax.broadcasted_iota(jnp.int32, (rows, held), 1)).astype(BF)


class Spread:
    def __init__(self, n, buf, layer, sems, started):
        self.depth = n // 4
        self.buf, self.layer, self.sems, self.started = buf, layer, sems, started
        self.z, self.y, self.c = place(n)
        self.core = index_of(self.z, self.y, 1 - self.c)
        self.side = index_of(self.z, 1 - self.y, self.c)
        self.order = near_first(self.depth)

    def copy(self, chunk, kind, slot, peer):
        ref = self.buf.at[self.layer, chunk]
        at = self.sems[2 * kind].at[self.layer, slot], self.sems[2 * kind + 1].at[self.layer, slot]
        return send(ref, ref, at[0], at[1], peer)

    def go(self, chunk, kind, slot, peer):
        copy = self.copy(chunk, kind, slot, peer)
        copy.start()
        self.started.append(copy)

    def chunk(self, k, y, c):
        return index_of((self.z - k + self.depth) % self.depth, y, c)

    def begin(self):
        mine = self.chunk(0, self.y, self.c)
        for k in reversed(self.order):
            self.go(mine, 0, k, index_of((self.z + k) % self.depth, self.y, self.c))
        self.go(mine, 1, 0, self.side)
        self.go(mine, 2, 0, self.core)

    def along_z(self):
        for k in self.order:
            chunk = self.chunk(k, self.y, self.c)
            self.copy(chunk, 0, k, self.core).wait_recv()
            self.go(chunk, 1, k, self.side)
            self.go(chunk, 2, k, self.core)

    def along_y(self):
        for k in [0] + self.order:
            chunk = self.chunk(k, 1 - self.y, self.c)
            self.copy(chunk, 1, k, self.side).wait_recv()
            self.go(chunk, 2, self.depth + k, self.core)

    def finish(self, out_ref):
        for k in [0] + self.order:
            self.copy(self.chunk(k, self.y, 1 - self.c), 2, k, self.core).wait_recv()
        for k in [0] + self.order:
            chunk = self.chunk(k, 1 - self.y, 1 - self.c)
            self.copy(chunk, 2, self.depth + k, self.core).wait_recv()
        n, rows = self.buf.shape[1:3]
        for i in range(0, n, 2):
            pair = [self.buf[self.layer, j].astype(F32) for j in (i, i + 1)]
            out_ref[self.layer, pl.ds(i * rows, 2 * rows), :] = jnp.concatenate(pair).astype(BF)


class Reduce:
    def __init__(self, n, part, layer, bufs, sems, started):
        self.n, self.depth = n, n // 4
        self.part, self.layer, self.bufs, self.sems, self.started = part, layer, bufs, sems, started
        self.z, self.y, self.c = place(n)
        self.core = index_of(self.z, self.y, 1 - self.c)
        self.side = index_of(self.z, 1 - self.y, self.c)
        self.order = near_first(self.depth)
        self.far = list(reversed(self.order)) + [0]

    def copy(self, kind, slot, peer):
        at = self.layer, slot
        out, into = self.bufs[2 * kind].at[at], self.bufs[2 * kind + 1].at[at]
        return send(out, into, self.sems[2 * kind].at[at], self.sems[2 * kind + 1].at[at], peer)

    def go(self, kind, slot, peer, value):
        self.bufs[2 * kind][self.layer, slot] = value.astype(BF)
        copy = self.copy(kind, slot, peer)
        copy.start()
        self.started.append(copy)

    def got(self, kind, slot, peer):
        self.copy(kind, slot, peer).wait_recv()
        return self.bufs[2 * kind + 1][self.layer, slot].astype(F32)

    def term(self, k, y, c):
        rows = self.part.shape[1] // self.n
        index = index_of((self.z + k) % self.depth, y, c)
        return self.part[self.layer, pl.ds(pl.multiple_of(index * rows, rows), rows), :]

    def to_core(self):
        for j, y in ((0, 1 - self.y), (1, self.y)):
            for k in self.far:
                self.go(0, j * self.depth + k, self.core, self.term(k, y, 1 - self.c))

    def to_y(self):
        for k in self.far:
            value = self.term(k, 1 - self.y, self.c) + self.got(0, k, self.core)
            self.go(1, k, self.side, value)

    def to_z(self):
        for k in self.far:
            total = self.term(k, self.y, self.c) + self.got(0, self.depth + k, self.core)
            total = total + self.got(1, k, self.side)
            if k:
                self.go(2, k, index_of((self.z + k) % self.depth, self.y, self.c), total)
        self.total = total

    def finish(self):
        total = self.total
        for k in self.order:
            total = total + self.got(2, k, self.core)
        return total


def forward_kernel(
    n, pairs, ids_ref, in_ref, goal_ref, bias_ref, enc_hbm, dec_hbm, x_ref, e_ref, a_ref,
    enc_ref, dec_ref, feat_ref, part_ref, xbuf, ebuf, cst, cin, yst, yin, zst, zin,
    enc_sem, dec_sem, *sems
):
    layers, held, width = in_ref.shape
    rows = ids_ref.shape[0]
    features = a_ref.shape[2]
    me = lax.axis_index("feat")
    enc_copies = [
        pltpu.make_async_copy(enc_hbm.at[i], enc_ref.at[i], enc_sem.at[i]) for i in range(layers)
    ]
    dec_copies = [
        pltpu.make_async_copy(dec_hbm.at[i], dec_ref.at[i], dec_sem.at[i])
        for i in range(len(pairs))
    ]
    hot = one_hot(ids_ref, rows, held)
    for layer in range(layers):
        xbuf[layer, me] = jnp.dot(hot, in_ref[layer], preferred_element_type=F32).astype(BF)
    greet(n)
    started = []
    gathers = [Spread(n, xbuf, layer, sems[:6], started) for layer in range(layers)]
    spreads = [Spread(n, ebuf, layer, sems[6:12], started) for layer in range(layers)]
    bufs = (cst, cin, yst, yin, zst, zin)
    reduces = [Reduce(n, part_ref, layer, bufs, sems[12:], started) for layer in range(layers)]
    for gather in gathers:
        gather.begin()
    for copy in enc_copies + dec_copies:
        copy.start()
    targets = [jnp.dot(hot, goal_ref[layer], preferred_element_type=F32) for layer in range(layers)]

    def encode(layer):
        gathers[layer].finish(x_ref)
        enc_copies[layer].wait()
        tile = min(256, features)

        @pl.loop(0, features // tile)
        def _(i):
            cols = pl.ds(pl.multiple_of(i * tile, tile), tile)
            value = jnp.dot(x_ref[layer], enc_ref[layer, :, cols], preferred_element_type=F32)
            value = value + bias_ref[pl.ds(layer, 1), cols]
            a_ref[layer, :, cols] = value
            feat_ref[layer, :, cols] = jnp.maximum(value, 0.0).astype(BF)

    def decode(target):
        mine = [index for index, pair in enumerate(pairs) if pair[1] == target]
        for index in mine:
            dec_copies[index].wait()
        tile = min(256, width)

        @pl.loop(0, width // tile)
        def _(i):
            cols = pl.ds(pl.multiple_of(i * tile, tile), tile)
            part_ref[target, :, cols] = sum(
                jnp.dot(feat_ref[pairs[p][0]], dec_ref[p, :, cols], preferred_element_type=F32)
                for p in mine
            )

        reduces[target].to_core()

    def errors(target):
        value = reduces[target].finish() - targets[target]
        ebuf[target, me] = value.astype(BF)
        spreads[target].begin()

    stages = (
        lambda layer: gathers[layer].along_z(),
        lambda layer: gathers[layer].along_y(),
        encode,
        decode,
        lambda layer: reduces[layer].to_y(),
        lambda layer: reduces[layer].to_z(),
        errors,
        lambda layer: spreads[layer].along_z(),
        lambda layer: spreads[layer].along_y(),
        lambda layer: spreads[layer].finish(e_ref),
    )
    steps = [(stage + 2 * layer, -layer, stage) for layer in range(layers) for stage in range(len(stages))]
    for _, layer, stage in sorted(steps):
        stages[stage](-layer)
    for copy in started:
        copy.wait_send()


def forward(n, pairs, ids, store_inputs, store_targets, enc_weight, enc_bias, dec_weight):
    layers, _, width = store_inputs.shape
    rows = ids.shape[0]
    features = enc_weight.shape[2]
    tokens = n * rows
    depth = n // 4
    dma = pltpu.SemaphoreType.DMA
    chunks = lambda count: pltpu.VMEM((layers, count, rows, width), BF)
    full = jax.ShapeDtypeStruct((layers, tokens, width), BF)
    vmem = pl.BlockSpec(memory_space=pltpu.VMEM)
    kept = pl.BlockSpec(memory_space=pl.ANY)
    one, two = [dma((layers, depth))] * 2, [dma((layers, 2 * depth))] * 2
    return pl.pallas_call(
        functools.partial(forward_kernel, n, pairs),
        out_shape=(full, full, jax.ShapeDtypeStruct((layers, tokens, features), F32)),
        in_specs=[pl.BlockSpec(memory_space=pltpu.SMEM)] + [vmem] * 3 + [kept] * 2,
        out_specs=(vmem,) * 3,
        scratch_shapes=[
            pltpu.VMEM(enc_weight.shape, BF),
            pltpu.VMEM(dec_weight.shape, BF),
            pltpu.VMEM((layers, tokens, features), BF),
            pltpu.VMEM((layers, tokens, width), F32),
        ]
        + [chunks(n)] * 2
        + [chunks(2 * depth)] * 2
        + [chunks(depth)] * 4
        + [dma((layers,)), dma((len(pairs),))]
        + (one + one + two) * 2
        + (two + one + one),
        compiler_params=pltpu.CompilerParams(
            collective_id=0, has_side_effects=True, vmem_limit_bytes=56 * 1024 * 1024
        ),
        name="forward",
    )(ids, store_inputs, store_targets, enc_bias, enc_weight, dec_weight)


def backward_kernel(pairs, scale, x_ref, e_ref, a_ref, w_ref, enc_ref, bias_ref, dec_ref, xt):
    layers = x_ref.shape[0]

    @pl.when(pl.program_id(0) == 0)
    def _():
        for layer in range(layers):
            xt[layer] = x_ref[layer].T

    for source in range(layers):
        active = a_ref[source]
        turned = jnp.maximum(active, 0.0).astype(BF).T
        grad = None
        for index, (first, target) in enumerate(pairs):
            if first != source:
                continue
            dec = jnp.dot(turned, e_ref[target], preferred_element_type=F32)
            dec_ref[index] = (scale * dec).astype(BF)
            back = lax.dot_general(
                e_ref[target], w_ref[index], (((1,), (1,)), ((), ())), preferred_element_type=F32
            )
            grad = back if grad is None else grad + back
        pre = jnp.where(active > 0, grad, 0.0) * scale
        bias_ref[pl.ds(source, 1), :] = jnp.sum(pre, axis=0, keepdims=True)
        enc = jnp.dot(xt[source], pre.astype(BF), preferred_element_type=F32)
        enc_ref[source] = enc.astype(BF)


def backward(pairs, scale, x, errors, preact, dec_weight):
    layers, tokens, width = x.shape
    features = preact.shape[2]
    tile = min(256, features)
    whole = pl.BlockSpec((layers, tokens, width), lambda i: (0, 0, 0))
    rows = pl.BlockSpec((len(pairs), tile, width), lambda i: (0, i, 0))
    return pl.pallas_call(
        functools.partial(backward_kernel, pairs, scale),
        grid=(features // tile,),
        out_shape=(
            jax.ShapeDtypeStruct((layers, width, features), BF),
            jax.ShapeDtypeStruct((layers, features), F32),
            jax.ShapeDtypeStruct((len(pairs), features, width), BF),
        ),
        in_specs=[whole, whole, pl.BlockSpec((layers, tokens, tile), lambda i: (0, 0, i)), rows],
        out_specs=(
            pl.BlockSpec((layers, width, tile), lambda i: (0, 0, i)),
            pl.BlockSpec((layers, tile), lambda i: (0, i)),
            rows,
        ),
        scratch_shapes=[pltpu.VMEM((layers, width, tokens), BF)],
        compiler_params=pltpu.CompilerParams(vmem_limit_bytes=48 * 1024 * 1024),
        name="backward",
    )(x, errors, preact, dec_weight)


def local(n, store_inputs, store_targets, row_ids, enc_weight, enc_bias, dec_weight):
    layers, width = enc_weight.shape[:2]
    rows = row_ids.shape[0]
    pairs = [(source, target) for source in range(layers) for target in range(source, layers)]
    scale = 1.0 / math.sqrt(rows * n)
    x, errors, preact = forward(
        n, pairs, row_ids, store_inputs, store_targets, enc_weight, enc_bias, dec_weight
    )
    return backward(pairs, scale, x, errors, preact, dec_weight)


def solution(mesh):
    in_specs = (
        P(None, ("group", "feat"), None),
        P(None, ("group", "feat"), None),
        P(("group", "feat")),
        P(None, None, "feat"),
        P(None, "feat"),
        P(None, "feat", None),
    )
    out_specs = (P("group", None, "feat"), P("group", "feat"), P("group", "feat", None))
    body = functools.partial(local, mesh.shape["feat"])
    return jax.shard_map(body, mesh=mesh, in_specs=in_specs, out_specs=out_specs, check_vma=False)
```

```python
import functools
import math

import jax
import jax.numpy as jnp
from jax import lax
from jax.experimental import pallas as pl
from jax.experimental.pallas import tpu as pltpu
from jax.sharding import PartitionSpec as P

BF = jnp.bfloat16
F32 = jnp.float32


def place(n):
    me = lax.axis_index("feat")
    return me // 4, (me // 2) % 2, me % 2


def index_of(z, y, c):
    return (z * 2 + y) * 2 + c


def near_first(depth):
    return sorted(range(1, depth), key=lambda k: min(k, depth - k))


def greet(n):
    depth = n // 4
    z, y, c = place(n)
    barrier = pltpu.get_barrier_semaphore()
    peers = [index_of(z, y, 1 - c), index_of(z, 1 - y, c)]
    peers += [index_of((z + k) % depth, y, c) for k in range(1, depth)]
    for peer in peers:
        pl.semaphore_signal(
            barrier, inc=1, device_id={"feat": peer}, device_id_type=pl.DeviceIdType.MESH
        )
    pl.semaphore_wait(barrier, len(peers))


def send(src, dst, send_sem, recv_sem, peer):
    return pltpu.make_async_remote_copy(
        src_ref=src,
        dst_ref=dst,
        send_sem=send_sem,
        recv_sem=recv_sem,
        device_id={"feat": peer},
        device_id_type=pl.DeviceIdType.MESH,
    )


def one_hot(ids_ref, rows, held):
    at = lax.broadcasted_iota(jnp.int32, (rows, held), 0)
    ids = jnp.zeros((rows, held), jnp.int32)
    for row in range(rows):
        ids = jnp.where(at == row, ids_ref[row], ids)
    return (ids == lax.broadcasted_iota(jnp.int32, (rows, held), 1)).astype(BF)


class Spread:
    def __init__(self, n, buf, layer, sems, started):
        self.depth = n // 4
        self.buf, self.layer, self.sems, self.started = buf, layer, sems, started
        self.z, self.y, self.c = place(n)
        self.core = index_of(self.z, self.y, 1 - self.c)
        self.side = index_of(self.z, 1 - self.y, self.c)
        self.order = near_first(self.depth)

    def copy(self, chunk, kind, slot, peer):
        ref = self.buf.at[self.layer, chunk]
        at = self.sems[2 * kind].at[self.layer, slot], self.sems[2 * kind + 1].at[self.layer, slot]
        return send(ref, ref, at[0], at[1], peer)

    def go(self, chunk, kind, slot, peer):
        copy = self.copy(chunk, kind, slot, peer)
        copy.start()
        self.started.append(copy)

    def chunk(self, k, y, c):
        return index_of((self.z - k + self.depth) % self.depth, y, c)

    def begin(self):
        mine = self.chunk(0, self.y, self.c)
        for k in reversed(self.order):
            self.go(mine, 0, k, index_of((self.z + k) % self.depth, self.y, self.c))
        self.go(mine, 1, 0, self.side)
        self.go(mine, 2, 0, self.core)

    def along_z(self):
        for k in self.order:
            chunk = self.chunk(k, self.y, self.c)
            self.copy(chunk, 0, k, self.core).wait_recv()
            self.go(chunk, 1, k, self.side)
            self.go(chunk, 2, k, self.core)

    def along_y(self):
        for k in [0] + self.order:
            chunk = self.chunk(k, 1 - self.y, self.c)
            self.copy(chunk, 1, k, self.side).wait_recv()
            self.go(chunk, 2, self.depth + k, self.core)

    def finish(self, out_ref):
        for k in [0] + self.order:
            self.copy(self.chunk(k, self.y, 1 - self.c), 2, k, self.core).wait_recv()
        for k in [0] + self.order:
            chunk = self.chunk(k, 1 - self.y, 1 - self.c)
            self.copy(chunk, 2, self.depth + k, self.core).wait_recv()
        n, rows = self.buf.shape[1:3]
        for i in range(0, n, 2):
            pair = [self.buf[self.layer, j].astype(F32) for j in (i, i + 1)]
            out_ref[self.layer, pl.ds(i * rows, 2 * rows), :] = jnp.concatenate(pair).astype(BF)


class Reduce:
    def __init__(self, n, part, layer, bufs, sems, started):
        self.n, self.depth = n, n // 4
        self.part, self.layer, self.bufs, self.sems, self.started = part, layer, bufs, sems, started
        self.z, self.y, self.c = place(n)
        self.core = index_of(self.z, self.y, 1 - self.c)
        self.side = index_of(self.z, 1 - self.y, self.c)
        self.order = near_first(self.depth)
        self.far = list(reversed(self.order)) + [0]

    def copy(self, kind, slot, peer):
        at = self.layer, slot
        out, into = self.bufs[2 * kind].at[at], self.bufs[2 * kind + 1].at[at]
        return send(out, into, self.sems[2 * kind].at[at], self.sems[2 * kind + 1].at[at], peer)

    def go(self, kind, slot, peer, value):
        self.bufs[2 * kind][self.layer, slot] = value.astype(BF)
        copy = self.copy(kind, slot, peer)
        copy.start()
        self.started.append(copy)

    def got(self, kind, slot, peer):
        self.copy(kind, slot, peer).wait_recv()
        return self.bufs[2 * kind + 1][self.layer, slot].astype(F32)

    def term(self, k, y, c):
        rows = self.part.shape[1] // self.n
        index = index_of((self.z + k) % self.depth, y, c)
        return self.part[self.layer, pl.ds(pl.multiple_of(index * rows, rows), rows), :]

    def to_core(self):
        for j, y in ((0, 1 - self.y), (1, self.y)):
            for k in self.far:
                self.go(0, j * self.depth + k, self.core, self.term(k, y, 1 - self.c))

    def to_y(self):
        for k in self.far:
            value = self.term(k, 1 - self.y, self.c) + self.got(0, k, self.core)
            self.go(1, k, self.side, value)

    def to_z(self):
        for k in self.far:
            total = self.term(k, self.y, self.c) + self.got(0, self.depth + k, self.core)
            total = total + self.got(1, k, self.side)
            if k:
                self.go(2, k, index_of((self.z + k) % self.depth, self.y, self.c), total)
        self.total = total

    def finish(self):
        total = self.total
        for k in self.order:
            total = total + self.got(2, k, self.core)
        return total


def forward_kernel(
    n, pairs, scale, ids_ref, in_ref, goal_ref, bias_ref, enc_hbm, dec_hbm, xt_ref, ft_ref, e_ref,
    pre_ref, x_ref, a_ref, enc_ref, dec_ref, feat_ref, part_ref, xbuf, ebuf, cst, cin, yst, yin, zst, zin,
    enc_sem, dec_sem, *sems
):
    layers, held, width = in_ref.shape
    rows = ids_ref.shape[0]
    features = a_ref.shape[2]
    me = lax.axis_index("feat")
    enc_copies = [
        pltpu.make_async_copy(enc_hbm.at[i], enc_ref.at[i], enc_sem.at[i]) for i in range(layers)
    ]
    dec_copies = [
        pltpu.make_async_copy(dec_hbm.at[i], dec_ref.at[i], dec_sem.at[i])
        for i in range(len(pairs))
    ]
    hot = one_hot(ids_ref, rows, held)
    for layer in range(layers):
        xbuf[layer, me] = jnp.dot(hot, in_ref[layer], preferred_element_type=F32).astype(BF)
    greet(n)
    started = []
    gathers = [Spread(n, xbuf, layer, sems[:6], started) for layer in range(layers)]
    spreads = [Spread(n, ebuf, layer, sems[6:12], started) for layer in range(layers)]
    bufs = (cst, cin, yst, yin, zst, zin)
    reduces = [Reduce(n, part_ref, layer, bufs, sems[12:], started) for layer in range(layers)]
    for gather in gathers:
        gather.begin()
    for copy in enc_copies + dec_copies:
        copy.start()
    targets = [jnp.dot(hot, goal_ref[layer], preferred_element_type=F32) for layer in range(layers)]

    def encode(layer):
        gathers[layer].finish(x_ref)
        enc_copies[layer].wait()
        tile = min(256, features)

        @pl.loop(0, features // tile)
        def _(i):
            cols = pl.ds(pl.multiple_of(i * tile, tile), tile)
            value = jnp.dot(x_ref[layer], enc_ref[layer, :, cols], preferred_element_type=F32)
            value = value + bias_ref[pl.ds(layer, 1), cols]
            a_ref[layer, :, cols] = value
            feat_ref[layer, :, cols] = jnp.maximum(value, 0.0).astype(BF)

    def decode(target):
        mine = [index for index, pair in enumerate(pairs) if pair[1] == target]
        for index in mine:
            dec_copies[index].wait()
        tile = min(256, width)

        @pl.loop(0, width // tile)
        def _(i):
            cols = pl.ds(pl.multiple_of(i * tile, tile), tile)
            part_ref[target, :, cols] = sum(
                jnp.dot(feat_ref[pairs[p][0]], dec_ref[p, :, cols], preferred_element_type=F32)
                for p in mine
            )

        reduces[target].to_core()

    def errors(target):
        value = reduces[target].finish() - targets[target]
        ebuf[target, me] = value.astype(BF)
        spreads[target].begin()

    def turn(layer):
        xt_ref[layer] = x_ref[layer].T
        ft_ref[layer] = feat_ref[layer].T

    def feature_grad(target):
        last = target == layers - 1
        tile = min(256, features)

        @pl.loop(0, features // tile)
        def _(i):
            cols = pl.ds(pl.multiple_of(i * tile, tile), tile)
            for index, (source, goal) in enumerate(pairs):
                if goal != target:
                    continue
                grad = lax.dot_general(
                    e_ref[target],
                    dec_ref[index, cols, :],
                    (((1,), (1,)), ((), ())),
                    preferred_element_type=F32,
                )
                if source < target:
                    grad = pre_ref[source, :, cols] + grad
                if last:
                    grad = jnp.where(a_ref[source, :, cols] > 0, grad, 0.0) * scale
                pre_ref[source, :, cols] = grad

    stages = (
        lambda layer: gathers[layer].along_z(),
        lambda layer: gathers[layer].along_y(),
        encode,
        decode,
        lambda layer: reduces[layer].to_y(),
        lambda layer: reduces[layer].to_z(),
        errors,
        lambda layer: spreads[layer].along_z(),
        lambda layer: spreads[layer].along_y(),
        lambda layer: spreads[layer].finish(e_ref),
    )
    steps = [
        (stage + 2 * layer, -layer, run)
        for layer in range(layers)
        for stage, run in enumerate(stages)
    ]
    steps += [(2 * layers + 4.5, -layer, turn) for layer in range(layers)]
    steps += [(10.5 + 2 * layer, -layer, feature_grad) for layer in range(layers)]
    for _, layer, run in sorted(steps, key=lambda step: step[:2]):
        run(-layer)
    for copy in started:
        copy.wait_send()


def forward(n, pairs, scale, ids, store_inputs, store_targets, enc_weight, enc_bias, dec_weight):
    layers, _, width = store_inputs.shape
    rows = ids.shape[0]
    features = enc_weight.shape[2]
    tokens = n * rows
    depth = n // 4
    dma = pltpu.SemaphoreType.DMA
    chunks = lambda count: pltpu.VMEM((layers, count, rows, width), BF)
    full = jax.ShapeDtypeStruct((layers, tokens, width), BF)
    vmem = pl.BlockSpec(memory_space=pltpu.VMEM)
    kept = pl.BlockSpec(memory_space=pl.ANY)
    one, two = [dma((layers, depth))] * 2, [dma((layers, 2 * depth))] * 2
    return pl.pallas_call(
        functools.partial(forward_kernel, n, pairs, scale),
        out_shape=(
            jax.ShapeDtypeStruct((layers, width, tokens), BF),
            jax.ShapeDtypeStruct((layers, features, tokens), BF),
            full,
            jax.ShapeDtypeStruct((layers, tokens, features), F32),
        ),
        in_specs=[pl.BlockSpec(memory_space=pltpu.SMEM)] + [vmem] * 3 + [kept] * 2,
        out_specs=(vmem,) * 4,
        scratch_shapes=[
            pltpu.VMEM((layers, tokens, width), BF),
            pltpu.VMEM((layers, tokens, features), F32),
            pltpu.VMEM(enc_weight.shape, BF),
            pltpu.VMEM(dec_weight.shape, BF),
            pltpu.VMEM((layers, tokens, features), BF),
            pltpu.VMEM((layers, tokens, width), F32),
        ]
        + [chunks(n)] * 2
        + [chunks(2 * depth)] * 2
        + [chunks(depth)] * 4
        + [dma((layers,)), dma((len(pairs),))]
        + (one + one + two) * 2
        + (two + one + one),
        compiler_params=pltpu.CompilerParams(
            collective_id=0, has_side_effects=True, vmem_limit_bytes=56 * 1024 * 1024
        ),
        name="forward",
    )(ids, store_inputs, store_targets, enc_bias, enc_weight, dec_weight)


def backward_kernel(pairs, scale, xt_ref, ft_ref, e_ref, pre_ref, enc_ref, bias_ref, dec_ref, half):
    layers = xt_ref.shape[0]

    @pl.when(pl.program_id(0) == 0)
    def _():
        for layer in range(layers):
            pre = pre_ref[layer]
            bias_ref[pl.ds(layer, 1), :] = jnp.sum(pre, axis=0, keepdims=True)
            half[layer] = pre.astype(BF)

    for index, (source, target) in enumerate(pairs):
        dec = jnp.dot(ft_ref[source], e_ref[target], preferred_element_type=F32)
        dec_ref[index] = (scale * dec).astype(BF)
    for layer in range(layers):
        enc = jnp.dot(xt_ref[layer], half[layer], preferred_element_type=F32)
        enc_ref[layer] = enc.astype(BF)


def backward(pairs, scale, xt, ft, errors, pre):
    layers, tokens, width = errors.shape
    features = pre.shape[2]
    steps = 4
    rows, tall = features // steps, width // steps
    tiles = lambda count, high, wide: pl.BlockSpec((count, high, wide), lambda i: (0, i, 0))
    whole = lambda wide: pl.BlockSpec((layers, tokens, wide), lambda i: (0, 0, 0))
    return pl.pallas_call(
        functools.partial(backward_kernel, pairs, scale),
        grid=(steps,),
        out_shape=(
            jax.ShapeDtypeStruct((layers, width, features), BF),
            jax.ShapeDtypeStruct((layers, features), F32),
            jax.ShapeDtypeStruct((len(pairs), features, width), BF),
        ),
        in_specs=[
            tiles(layers, tall, tokens), tiles(layers, rows, tokens), whole(width), whole(features)
        ],
        out_specs=(
            tiles(layers, tall, features),
            pl.BlockSpec((layers, features), lambda i: (0, 0)),
            tiles(len(pairs), rows, width),
        ),
        scratch_shapes=[pltpu.VMEM((layers, tokens, features), BF)],
        compiler_params=pltpu.CompilerParams(vmem_limit_bytes=67_043_328),
        name="backward",
    )(xt, ft, errors, pre)


def local(n, store_inputs, store_targets, row_ids, enc_weight, enc_bias, dec_weight):
    layers, width = enc_weight.shape[:2]
    rows = row_ids.shape[0]
    pairs = [(source, target) for source in range(layers) for target in range(source, layers)]
    scale = 1.0 / math.sqrt(rows * n)
    args = row_ids, store_inputs, store_targets, enc_weight, enc_bias, dec_weight
    return backward(pairs, scale, *forward(n, pairs, scale, *args))


def solution(mesh):
    in_specs = (
        P(None, ("group", "feat"), None),
        P(None, ("group", "feat"), None),
        P(("group", "feat")),
        P(None, None, "feat"),
        P(None, "feat"),
        P(None, "feat", None),
    )
    out_specs = (P("group", None, "feat"), P("group", "feat"), P("group", "feat", None))
    body = functools.partial(local, mesh.shape["feat"])
    return jax.shard_map(body, mesh=mesh, in_specs=in_specs, out_specs=out_specs, check_vma=False)
```

```python
import functools
import math

import jax
import jax.numpy as jnp
from jax import lax
from jax.experimental import pallas as pl
from jax.experimental.pallas import tpu as pltpu
from jax.sharding import PartitionSpec as P

BF = jnp.bfloat16
F32 = jnp.float32


def place(n):
    me = lax.axis_index("feat")
    return me // 4, (me // 2) % 2, me % 2


def index_of(z, y, c):
    return (z * 2 + y) * 2 + c


def near_first(depth):
    return sorted(range(1, depth), key=lambda k: min(k, depth - k))


def greet(n):
    depth = n // 4
    z, y, c = place(n)
    barrier = pltpu.get_barrier_semaphore()
    peers = [index_of(z, y, 1 - c), index_of(z, 1 - y, c)]
    peers += [index_of((z + k) % depth, y, c) for k in range(1, depth)]
    for peer in peers:
        pl.semaphore_signal(
            barrier, inc=1, device_id={"feat": peer}, device_id_type=pl.DeviceIdType.MESH
        )
    pl.semaphore_wait(barrier, len(peers))


def send(src, dst, send_sem, recv_sem, peer):
    return pltpu.make_async_remote_copy(
        src_ref=src,
        dst_ref=dst,
        send_sem=send_sem,
        recv_sem=recv_sem,
        device_id={"feat": peer},
        device_id_type=pl.DeviceIdType.MESH,
    )


def one_hot(ids_ref, rows, held):
    at = lax.broadcasted_iota(jnp.int32, (rows, held), 0)
    ids = jnp.zeros((rows, held), jnp.int32)
    for row in range(rows):
        ids = jnp.where(at == row, ids_ref[row], ids)
    return (ids == lax.broadcasted_iota(jnp.int32, (rows, held), 1)).astype(BF)


class Spread:
    def __init__(self, n, buf, layer, sems, started):
        self.depth = n // 4
        self.buf, self.layer, self.sems, self.started = buf, layer, sems, started
        self.z, self.y, self.c = place(n)
        self.core = index_of(self.z, self.y, 1 - self.c)
        self.side = index_of(self.z, 1 - self.y, self.c)
        self.order = near_first(self.depth)

    def copy(self, chunk, kind, slot, peer):
        ref = self.buf.at[self.layer, chunk]
        at = self.sems[2 * kind].at[self.layer, slot], self.sems[2 * kind + 1].at[self.layer, slot]
        return send(ref, ref, at[0], at[1], peer)

    def go(self, chunk, kind, slot, peer):
        copy = self.copy(chunk, kind, slot, peer)
        copy.start()
        self.started.append(copy)

    def chunk(self, k, y, c):
        return index_of((self.z - k + self.depth) % self.depth, y, c)

    def begin(self):
        mine = self.chunk(0, self.y, self.c)
        for k in reversed(self.order):
            self.go(mine, 0, k, index_of((self.z + k) % self.depth, self.y, self.c))
        self.go(mine, 1, 0, self.side)
        self.go(mine, 2, 0, self.core)

    def along_z(self):
        for k in self.order:
            chunk = self.chunk(k, self.y, self.c)
            self.copy(chunk, 0, k, self.core).wait_recv()
            self.go(chunk, 1, k, self.side)
            self.go(chunk, 2, k, self.core)

    def along_y(self):
        for k in [0] + self.order:
            chunk = self.chunk(k, 1 - self.y, self.c)
            self.copy(chunk, 1, k, self.side).wait_recv()
            self.go(chunk, 2, self.depth + k, self.core)

    def finish(self, out_ref):
        for k in [0] + self.order:
            self.copy(self.chunk(k, self.y, 1 - self.c), 2, k, self.core).wait_recv()
        for k in [0] + self.order:
            chunk = self.chunk(k, 1 - self.y, 1 - self.c)
            self.copy(chunk, 2, self.depth + k, self.core).wait_recv()
        n, rows = self.buf.shape[1:3]
        for i in range(0, n, 2):
            pair = [self.buf[self.layer, j].astype(F32) for j in (i, i + 1)]
            out_ref[self.layer, pl.ds(i * rows, 2 * rows), :] = jnp.concatenate(pair).astype(BF)


class Reduce:
    def __init__(self, n, part, layer, bufs, sems, started):
        self.n, self.depth = n, n // 4
        self.part, self.layer, self.bufs, self.sems, self.started = part, layer, bufs, sems, started
        self.z, self.y, self.c = place(n)
        self.core = index_of(self.z, self.y, 1 - self.c)
        self.side = index_of(self.z, 1 - self.y, self.c)
        self.order = near_first(self.depth)
        self.far = list(reversed(self.order)) + [0]

    def copy(self, kind, slot, peer):
        at = self.layer, slot
        out, into = self.bufs[2 * kind].at[at], self.bufs[2 * kind + 1].at[at]
        return send(out, into, self.sems[2 * kind].at[at], self.sems[2 * kind + 1].at[at], peer)

    def go(self, kind, slot, peer, value):
        self.bufs[2 * kind][self.layer, slot] = value.astype(BF)
        copy = self.copy(kind, slot, peer)
        copy.start()
        self.started.append(copy)

    def got(self, kind, slot, peer):
        self.copy(kind, slot, peer).wait_recv()
        return self.bufs[2 * kind + 1][self.layer, slot].astype(F32)

    def term(self, k, y, c):
        rows = self.part.shape[1] // self.n
        index = index_of((self.z + k) % self.depth, y, c)
        return self.part[self.layer, pl.ds(pl.multiple_of(index * rows, rows), rows), :]

    def to_core(self):
        for j, y in ((0, 1 - self.y), (1, self.y)):
            for k in self.far:
                self.go(0, j * self.depth + k, self.core, self.term(k, y, 1 - self.c))

    def to_y(self):
        for k in self.far:
            value = self.term(k, 1 - self.y, self.c) + self.got(0, k, self.core)
            self.go(1, k, self.side, value)

    def to_z(self):
        for k in self.far:
            total = self.term(k, self.y, self.c) + self.got(0, self.depth + k, self.core)
            total = total + self.got(1, k, self.side)
            if k:
                self.go(2, k, index_of((self.z + k) % self.depth, self.y, self.c), total)
        self.total = total

    def finish(self):
        total = self.total
        for k in self.order:
            total = total + self.got(2, k, self.core)
        return total


def forward_kernel(
    n, pairs, scale, ids_ref, in_ref, goal_ref, bias_ref, enc_hbm, dec_hbm, xt_ref, ft_ref, e_ref,
    pre_ref, x_ref, a_ref, enc_ref, dec_ref, feat_ref, part_ref, xbuf, ebuf, cst, cin, yst, yin, zst, zin,
    enc_sem, dec_sem, *sems
):
    layers, held, width = in_ref.shape
    rows = ids_ref.shape[0]
    features = a_ref.shape[2]
    me = lax.axis_index("feat")
    enc_copies = [
        pltpu.make_async_copy(enc_hbm.at[i], enc_ref.at[i], enc_sem.at[i]) for i in range(layers)
    ]
    dec_copies = [
        pltpu.make_async_copy(dec_hbm.at[i], dec_ref.at[i], dec_sem.at[i])
        for i in range(len(pairs))
    ]
    hot = one_hot(ids_ref, rows, held)
    for layer in range(layers):
        xbuf[layer, me] = jnp.dot(hot, in_ref[layer], preferred_element_type=F32).astype(BF)
    greet(n)
    started = []
    gathers = [Spread(n, xbuf, layer, sems[:6], started) for layer in range(layers)]
    spreads = [Spread(n, ebuf, layer, sems[6:12], started) for layer in range(layers)]
    bufs = (cst, cin, yst, yin, zst, zin)
    reduces = [Reduce(n, part_ref, layer, bufs, sems[12:], started) for layer in range(layers)]
    for gather in gathers:
        gather.begin()
    for copy in enc_copies + dec_copies:
        copy.start()
    targets = [jnp.dot(hot, goal_ref[layer], preferred_element_type=F32) for layer in range(layers)]

    def encode(layer):
        gathers[layer].finish(x_ref)
        enc_copies[layer].wait()
        tile = min(512, features)

        @pl.loop(0, features // tile)
        def _(i):
            cols = pl.ds(pl.multiple_of(i * tile, tile), tile)
            value = jnp.dot(x_ref[layer], enc_ref[layer, :, cols], preferred_element_type=F32)
            value = value + bias_ref[pl.ds(layer, 1), cols]
            a_ref[layer, :, cols] = value
            feat_ref[layer, :, cols] = jnp.maximum(value, 0.0).astype(BF)

    def decode(target):
        mine = [index for index, pair in enumerate(pairs) if pair[1] == target]
        for index in mine:
            dec_copies[index].wait()
        tile = min(512, width)

        @pl.loop(0, width // tile)
        def _(i):
            cols = pl.ds(pl.multiple_of(i * tile, tile), tile)
            part_ref[target, :, cols] = sum(
                jnp.dot(feat_ref[pairs[p][0]], dec_ref[p, :, cols], preferred_element_type=F32)
                for p in mine
            )

        reduces[target].to_core()

    def errors(target):
        value = reduces[target].finish() - targets[target]
        ebuf[target, me] = value.astype(BF)
        spreads[target].begin()

    def turn(layer):
        xt_ref[layer] = x_ref[layer].T
        ft_ref[layer] = feat_ref[layer].T

    def feature_grad(target):
        last = target == layers - 1
        tile = min(512, features)

        @pl.loop(0, features // tile)
        def _(i):
            cols = pl.ds(pl.multiple_of(i * tile, tile), tile)
            for index, (source, goal) in enumerate(pairs):
                if goal != target:
                    continue
                grad = lax.dot_general(
                    e_ref[target],
                    dec_ref[index, cols, :],
                    (((1,), (1,)), ((), ())),
                    preferred_element_type=F32,
                )
                if source < target:
                    grad = pre_ref[source, :, cols] + grad
                if last:
                    grad = jnp.where(a_ref[source, :, cols] > 0, grad, 0.0) * scale
                pre_ref[source, :, cols] = grad

    stages = (
        lambda layer: gathers[layer].along_z(),
        lambda layer: gathers[layer].along_y(),
        encode,
        decode,
        lambda layer: reduces[layer].to_y(),
        lambda layer: reduces[layer].to_z(),
        errors,
        lambda layer: spreads[layer].along_z(),
        lambda layer: spreads[layer].along_y(),
        lambda layer: spreads[layer].finish(e_ref),
    )
    steps = [
        (stage + layer, -layer, run)
        for layer in range(layers)
        for stage, run in enumerate(stages)
    ]
    steps += [(layers + 5.5, -layer, turn) for layer in range(layers)]
    steps += [(9.5 + layer, -layer, feature_grad) for layer in range(layers)]
    for _, layer, run in sorted(steps, key=lambda step: step[:2]):
        run(-layer)
    for copy in started:
        copy.wait_send()


def forward(n, pairs, scale, ids, store_inputs, store_targets, enc_weight, enc_bias, dec_weight):
    layers, _, width = store_inputs.shape
    rows = ids.shape[0]
    features = enc_weight.shape[2]
    tokens = n * rows
    depth = n // 4
    dma = pltpu.SemaphoreType.DMA
    chunks = lambda count: pltpu.VMEM((layers, count, rows, width), BF)
    full = jax.ShapeDtypeStruct((layers, tokens, width), BF)
    vmem = pl.BlockSpec(memory_space=pltpu.VMEM)
    kept = pl.BlockSpec(memory_space=pl.ANY)
    one, two = [dma((layers, depth))] * 2, [dma((layers, 2 * depth))] * 2
    return pl.pallas_call(
        functools.partial(forward_kernel, n, pairs, scale),
        out_shape=(
            jax.ShapeDtypeStruct((layers, width, tokens), BF),
            jax.ShapeDtypeStruct((layers, features, tokens), BF),
            full,
            jax.ShapeDtypeStruct((layers, tokens, features), F32),
        ),
        in_specs=[pl.BlockSpec(memory_space=pltpu.SMEM)] + [vmem] * 3 + [kept] * 2,
        out_specs=(vmem,) * 4,
        scratch_shapes=[
            pltpu.VMEM((layers, tokens, width), BF),
            pltpu.VMEM((layers, tokens, features), F32),
            pltpu.VMEM(enc_weight.shape, BF),
            pltpu.VMEM(dec_weight.shape, BF),
            pltpu.VMEM((layers, tokens, features), BF),
            pltpu.VMEM((layers, tokens, width), F32),
        ]
        + [chunks(n)] * 2
        + [chunks(2 * depth)] * 2
        + [chunks(depth)] * 4
        + [dma((layers,)), dma((len(pairs),))]
        + (one + one + two) * 2
        + (two + one + one),
        compiler_params=pltpu.CompilerParams(
            collective_id=0, has_side_effects=True, vmem_limit_bytes=56 * 1024 * 1024
        ),
        name="forward",
    )(ids, store_inputs, store_targets, enc_bias, enc_weight, dec_weight)


def backward_kernel(pairs, scale, xt_ref, ft_ref, e_ref, pre_ref, enc_ref, bias_ref, dec_ref, half):
    layers = xt_ref.shape[0]

    @pl.when(pl.program_id(0) == 0)
    def _():
        for layer in range(layers):
            pre = pre_ref[layer]
            bias_ref[pl.ds(layer, 1), :] = jnp.sum(pre, axis=0, keepdims=True)
            half[layer] = pre.astype(BF)

    for index, (source, target) in enumerate(pairs):
        dec = jnp.dot(ft_ref[source], e_ref[target], preferred_element_type=F32)
        dec_ref[index] = (scale * dec).astype(BF)
    for layer in range(layers):
        enc = jnp.dot(xt_ref[layer], half[layer], preferred_element_type=F32)
        enc_ref[layer] = enc.astype(BF)


def backward(pairs, scale, xt, ft, errors, pre):
    layers, tokens, width = errors.shape
    features = pre.shape[2]
    steps = 4
    rows, tall = features // steps, width // steps
    tiles = lambda count, high, wide: pl.BlockSpec((count, high, wide), lambda i: (0, i, 0))
    whole = lambda wide: pl.BlockSpec((layers, tokens, wide), lambda i: (0, 0, 0))
    return pl.pallas_call(
        functools.partial(backward_kernel, pairs, scale),
        grid=(steps,),
        out_shape=(
            jax.ShapeDtypeStruct((layers, width, features), BF),
            jax.ShapeDtypeStruct((layers, features), F32),
            jax.ShapeDtypeStruct((len(pairs), features, width), BF),
        ),
        in_specs=[
            tiles(layers, tall, tokens), tiles(layers, rows, tokens), whole(width), whole(features)
        ],
        out_specs=(
            tiles(layers, tall, features),
            pl.BlockSpec((layers, features), lambda i: (0, 0)),
            tiles(len(pairs), rows, width),
        ),
        scratch_shapes=[pltpu.VMEM((layers, tokens, features), BF)],
        compiler_params=pltpu.CompilerParams(vmem_limit_bytes=67_043_328),
        name="backward",
    )(xt, ft, errors, pre)


def local(n, store_inputs, store_targets, row_ids, enc_weight, enc_bias, dec_weight):
    layers, width = enc_weight.shape[:2]
    rows = row_ids.shape[0]
    pairs = [(source, target) for source in range(layers) for target in range(source, layers)]
    scale = 1.0 / math.sqrt(rows * n)
    args = row_ids, store_inputs, store_targets, enc_weight, enc_bias, dec_weight
    return backward(pairs, scale, *forward(n, pairs, scale, *args))


def solution(mesh):
    in_specs = (
        P(None, ("group", "feat"), None),
        P(None, ("group", "feat"), None),
        P(("group", "feat")),
        P(None, None, "feat"),
        P(None, "feat"),
        P(None, "feat", None),
    )
    out_specs = (P("group", None, "feat"), P("group", "feat"), P("group", "feat", None))
    body = functools.partial(local, mesh.shape["feat"])
    return jax.shard_map(body, mesh=mesh, in_specs=in_specs, out_specs=out_specs, check_vma=False)
```
